32 devices in a mesh: tm: 32 (over z, y, x, core).
Axes of the slice: x: 2, y: 2, z: 4, core: 2. Of those that a mesh axis runs over, the one named last changes fastest.
Arguments:
- stream: bfloat16 [65536, 64], P('tm'), may hold values from -6 to 6
- w_in: bfloat16 [64, 256], replicated, may hold values from -0.75 to 0.75
- w_conv: bfloat16 [4, 2, 256, 512], replicated, may hold values from -0.25 to 0.25
- w_residual: bfloat16 [3, 256, 256], replicated, may hold values from -0.375 to 0.375
- w_skip: bfloat16 [4, 256, 256], replicated, may hold values from -0.375 to 0.375
- w_out: bfloat16 [256, 64], replicated, may hold values from -0.375 to 0.375
- grad_pred: bfloat16 [65536, 64], P('tm'), may hold values from -0.0234375 to 0.0234375
Outputs:
- prediction: bfloat16 [65536, 64], P('tm')
- grad_w_in: float32 [64, 256], replicated
- grad_w_conv: float32 [4, 2, 256, 512], replicated
- grad_w_residual: float32 [3, 256, 256], replicated
- grad_w_skip: float32 [4, 256, 256], replicated
- grad_w_out: float32 [256, 64], replicated
The draws below stay inside these ranges and needn't reach their ends.
All inputs are finite; a program needn't handle non-finite values.
Results may differ from the reference program's by a relative error of at most 0.012.
Values may be sent and summed in bfloat16 or wider, within the bound.
A program may use at most 128 MiB of HBM per device.

```python
import jax
import jax.numpy as jnp

FEAT = 64
RES = 256
GATE = 512
SKIP = 256
LAYERS = 4
TOK_DEV = 2048
TOKENS = 65536


def block_scale(stream_key, shape, split, low, top_value):
    loudness, own = 1.0, jax.random.fold_in(stream_key, 6)
    for axis_at, blocks in split:
        draws = jnp.exp(jax.random.uniform(jax.random.fold_in(own, axis_at), (blocks,), jnp.float32, low / len(split), top_value / len(split)))
        loudness = loudness * jnp.repeat(draws, shape[axis_at] // blocks).reshape([-1 if axis == axis_at else 1 for axis in range(len(shape))])
    return loudness


def centred(stream_key, shape, scale, most, split=(), held_as=jnp.bfloat16):
    result = jax.random.normal(stream_key, shape, jnp.float32) * scale
    if len(split) > 0:
        result = block_scale(stream_key, shape, split, -0.22, 0.18) * result
    return jnp.clip(result, min=-most, max=most).astype(held_as)


def setup_inputs(seed: int = 0) -> dict:
    seeds = jax.random.split(jax.random.key(seed), 8)
    return {
        "stream": centred(seeds[0], (TOKENS, FEAT), 1.0, 6.0, ((0, 32),)),
        "w_in": centred(seeds[1], (FEAT, RES), FEAT ** -0.5, 0.75),
        "w_conv": centred(seeds[2], (LAYERS, 2, RES, GATE), (2 * RES) ** -0.5, 0.25),
        "w_residual": centred(seeds[3], (LAYERS - 1, RES, RES), RES ** -0.5, 0.375),
        "w_skip": centred(seeds[4], (LAYERS, RES, SKIP), RES ** -0.5, 0.375),
        "w_out": centred(seeds[5], (SKIP, FEAT), SKIP ** -0.5, 0.375),
        "grad_pred": centred(seeds[6], (TOKENS, FEAT), (TOKENS ** -0.5), 0.0234375, ((0, 32),)),
    }


def lag_rows(h, dist):
    return jnp.concatenate([jnp.zeros((dist, h.shape[1]), h.dtype), h[:h.shape[0] - dist]], axis=0)


def unlag_rows(moved, dist):
    return jnp.concatenate([moved[dist:], jnp.zeros((dist, moved.shape[1]), moved.dtype)], axis=0)


def tdot(left, right):
    return jnp.dot(left.T, right, preferred_element_type=jnp.float32)


def reference(stream, w_in, w_conv, w_residual, w_skip, w_out, grad_pred):
    width = w_in.shape[1]
    h = jnp.dot(stream, w_in, preferred_element_type=jnp.float32).astype(jnp.bfloat16)
    skip = jnp.zeros((stream.shape[0], w_skip.shape[2]), jnp.float32)
    saved = []
    for layer in range(LAYERS):
        dist = TOK_DEV * 2 ** layer // 4
        lagged = lag_rows(h, dist)
        z = jnp.dot(lagged, w_conv[layer, 0], preferred_element_type=jnp.float32) + jnp.dot(h, w_conv[layer, 1], preferred_element_type=jnp.float32)
        gated = (jnp.tanh(z[:, :width]) * jax.nn.sigmoid(z[:, width:])).astype(jnp.bfloat16)
        skip = skip + jnp.dot(gated, w_skip[layer], preferred_element_type=jnp.float32)
        saved.append((h, lagged, z, gated))
        if layer < LAYERS - 1:
            h = (h.astype(jnp.float32) + jnp.dot(gated, w_residual[layer], preferred_element_type=jnp.float32)).astype(jnp.bfloat16)
    sig_skip = jax.nn.sigmoid(skip)
    active = (skip * sig_skip).astype(jnp.bfloat16)
    prediction = jnp.dot(active, w_out, preferred_element_type=jnp.float32).astype(jnp.bfloat16)
    grad_w_out = tdot(active, grad_pred)
    dact = jnp.dot(grad_pred, w_out.T, preferred_element_type=jnp.float32)
    dskip = (dact * sig_skip * (1.0 + skip * (1.0 - sig_skip))).astype(jnp.bfloat16)
    grad_conv = [None] * LAYERS
    grad_res = [None] * (LAYERS - 1)
    grad_skip = [None] * LAYERS
    dh = None
    for layer in reversed(range(LAYERS)):
        dist = TOK_DEV * 2 ** layer // 4
        h_l, lagged, z, gated = saved[layer]
        dg = jnp.dot(dskip, w_skip[layer].T, preferred_element_type=jnp.float32)
        grad_skip[layer] = tdot(gated, dskip)
        if layer < LAYERS - 1:
            dh_b = dh.astype(jnp.bfloat16)
            dg = dg + jnp.dot(dh_b, w_residual[layer].T, preferred_element_type=jnp.float32)
            grad_res[layer] = tdot(gated, dh_b)
        tanh_part = jnp.tanh(z[:, :width])
        sig_part = jax.nn.sigmoid(z[:, width:])
        dz = jnp.concatenate([dg * sig_part * (1.0 - tanh_part * tanh_part), dg * tanh_part * sig_part * (1.0 - sig_part)], axis=1).astype(jnp.bfloat16)
        grad_conv[layer] = jnp.stack([tdot(lagged, dz), tdot(h_l, dz)])
        new_dh = jnp.dot(dz, w_conv[layer, 1].T, preferred_element_type=jnp.float32) + unlag_rows(jnp.dot(dz, w_conv[layer, 0].T, preferred_element_type=jnp.float32), dist)
        if layer < LAYERS - 1:
            new_dh = new_dh + dh
        dh = new_dh
    grad_w_in = tdot(stream, dh.astype(jnp.bfloat16))
    return (prediction, grad_w_in, jnp.stack(grad_conv), jnp.stack(grad_res), jnp.stack(grad_skip), grad_w_out)
```

```python
import jax
import jax.numpy as jnp
from jax import lax
from jax.sharding import PartitionSpec as P


def shifted(x, axis, by):
    peers = lax.axis_size(axis)
    pairs = [(i, i + by) for i in range(peers) if 0 <= i + by < peers]
    return lax.ppermute(x, axis, pairs)


def tdot(left, right):
    return lax.dot_general(
        left, right, (((0,), (0,)), ((), ())), preferred_element_type=jnp.float32
    )


def unlag_rows(moved, dist):
    rows = moved.shape[0]
    if dist < rows:
        local = jnp.concatenate(
            [moved[dist:], jnp.zeros((dist, moved.shape[1]), jnp.float32)], axis=0
        )
        incoming = shifted(moved[:dist].astype(jnp.bfloat16), "tm", -1).astype(jnp.float32)
        return local + jnp.concatenate(
            [jnp.zeros((rows - dist, moved.shape[1]), jnp.float32), incoming], axis=0
        )
    if dist == rows:
        return shifted(moved.astype(jnp.bfloat16), "tm", -1).astype(moved.dtype)
    return shifted(moved.astype(jnp.bfloat16), "tm", -(dist // rows)).astype(moved.dtype)


def conv_pre(h, lagged, taps):
    return jnp.dot(lagged, taps[0], preferred_element_type=jnp.float32) + jnp.dot(
        h, taps[1], preferred_element_type=jnp.float32
    )


def gate(z, width):
    return (jnp.tanh(z[:, :width]) * jax.nn.sigmoid(z[:, width:])).astype(jnp.bfloat16)


def advance(h, gated, w):
    return (
        h.astype(jnp.float32) + jnp.dot(gated, w, preferred_element_type=jnp.float32)
    ).astype(jnp.bfloat16)


def take(runs, first, count):
    parts = []
    at, last = first, first + count
    for start, block in runs:
        stop = start + block.shape[0]
        if start <= at < stop:
            end = min(stop, last)
            parts.append(block[at - start : end - start])
            at = end
        if at == last:
            break
    assert at == last
    return parts[0] if len(parts) == 1 else jnp.concatenate(parts, axis=0)


def needed(dists, rows):
    spans = [(0, rows)]
    for dist in reversed(dists):
        spans = merged(spans + [(lo - dist, hi - dist) for lo, hi in spans])
    out = []
    for lo, hi in spans:
        if lo < 0:
            out.append((lo, min(hi, 0) - lo))
    return out


def merged(spans):
    out = []
    for lo, hi in sorted(spans):
        if out and lo <= out[-1][1]:
            out[-1] = (out[-1][0], max(out[-1][1], hi))
        else:
            out.append((lo, hi))
    return out


def body(stream, w_in, w_conv, w_residual, w_skip, w_out, grad_pred):
    width = w_in.shape[1]
    rows = stream.shape[0]
    layers = w_conv.shape[0]
    skip_width = w_skip.shape[2]
    dists = [rows * 2**layer // 4 for layer in range(layers)]
    reach = sum(dists)
    blocks = -(-reach // rows)
    pieces = []
    for back in range(blocks, 0, -1):
        want = min(rows, reach - (back - 1) * rows)
        pieces.append(shifted(stream[rows - want :], "tm", back))
    past = jnp.dot(
        jnp.concatenate(pieces, axis=0), w_in, preferred_element_type=jnp.float32
    ).astype(jnp.bfloat16)
    h = jnp.dot(stream, w_in, preferred_element_type=jnp.float32).astype(jnp.bfloat16)
    skip = jnp.zeros((rows, skip_width), jnp.float32)
    saved = []
    runs = [(-reach, past)]
    for layer in range(layers):
        dist = dists[layer]
        lagged = take(runs + [(0, h)], -dist, rows)
        z = conv_pre(h, lagged, w_conv[layer])
        gated = gate(z, width)
        skip = skip + jnp.dot(gated, w_skip[layer], preferred_element_type=jnp.float32)
        saved.append((h, lagged, z, gated))
        if layer < layers - 1:
            runs_next = []
            for first, count in needed(dists[layer + 1 :], rows):
                old = take(runs, first, count)
                z_old = conv_pre(old, take(runs, first - dist, count), w_conv[layer])
                runs_next.append((first, advance(old, gate(z_old, width), w_residual[layer])))
            h = advance(h, gated, w_residual[layer])
            runs = runs_next
    sig_skip = jax.nn.sigmoid(skip)
    active = (skip * sig_skip).astype(jnp.bfloat16)
    prediction = jnp.dot(active, w_out, preferred_element_type=jnp.float32).astype(jnp.bfloat16)
    local_out = tdot(grad_pred, active)
    dact = jnp.dot(grad_pred, w_out.T, preferred_element_type=jnp.float32)
    dskip = (dact * sig_skip * (1.0 + skip * (1.0 - sig_skip))).astype(jnp.bfloat16)
    grad_conv = [None] * layers
    grad_res = [None] * (layers - 1)
    grad_skip = [None] * layers
    dh = None
    waiting = []
    for layer in reversed(range(layers)):
        dist = rows * 2**layer // 4
        h_l, lagged, z, gated = saved[layer]
        dg = jnp.dot(dskip, w_skip[layer].T, preferred_element_type=jnp.float32)
        part_skip = tdot(gated, dskip)
        if layer < layers - 1:
            dh_b = dh.astype(jnp.bfloat16)
            dg = dg + jnp.dot(dh_b, w_residual[layer].T, preferred_element_type=jnp.float32)
            part_res = tdot(gated, dh_b)
        tanh_part = jnp.tanh(z[:, :width])
        sig_part = jax.nn.sigmoid(z[:, width:])
        dz = jnp.concatenate(
            [
                dg * sig_part * (1.0 - tanh_part * tanh_part),
                dg * tanh_part * sig_part * (1.0 - sig_part),
            ],
            axis=1,
        ).astype(jnp.bfloat16)
        part_conv = jnp.stack([tdot(lagged, dz), tdot(h_l, dz)])
        mine = [part_conv, part_skip]
        if layer < layers - 1:
            mine.append(part_res)
        else:
            mine[1] = jnp.concatenate([part_skip, local_out], axis=0)
        waiting.append((layer, mine))
        new_dh = jnp.dot(dz, w_conv[layer, 1].T, preferred_element_type=jnp.float32) + unlag_rows(
            jnp.dot(dz, w_conv[layer, 0].T, preferred_element_type=jnp.float32), dist
        )
        if layer < layers - 1:
            new_dh = new_dh + dh
        dh = new_dh
    local_in = tdot(stream, dh.astype(jnp.bfloat16))
    before = None
    for layer, mine in waiting:
        if layer == 0:
            mine = [mine[0], jnp.concatenate([mine[1], local_in], axis=0)] + mine[2:]
        sent = [part.astype(jnp.bfloat16) for part in mine]
        if before is not None:
            sent, before = lax.optimization_barrier((sent, before))
        before = lax.psum(sent, "tm")
        got = [part.astype(jnp.float32) for part in before]
        grad_conv[layer], grad_skip[layer] = got[0], got[1][:width]
        if layer < layers - 1:
            grad_res[layer] = got[2]
        else:
            grad_w_out = got[1][width:].T
        if layer == 0:
            grad_w_in = got[1][width:]
    stacked_conv, stacked_skip = jnp.stack(grad_conv), jnp.stack(grad_skip)
    stacked_res = jnp.stack(grad_res)
    return (prediction, grad_w_in, stacked_conv, stacked_res, stacked_skip, grad_w_out)


def solution(mesh):
    placed = (P("tm", None), P(), P(), P(), P(), P(), P("tm", None))
    return jax.shard_map(
        body,
        mesh=mesh,
        in_specs=placed,
        out_specs=(P("tm", None), P(), P(), P(), P(), P()),
        check_vma=False,
    )
```

```python
import jax
import jax.numpy as jnp
from jax import lax
from jax.sharding import PartitionSpec as P


def shifted(x, axis, by):
    peers = lax.axis_size(axis)
    pairs = [(i, i + by) for i in range(peers) if 0 <= i + by < peers]
    return lax.ppermute(x, axis, pairs)


def tdot(left, right):
    return lax.dot_general(
        left, right, (((0,), (0,)), ((), ())), preferred_element_type=jnp.float32
    )


def lag_rows(h, dist):
    rows = h.shape[0]
    if dist < rows:
        recent = shifted(h[rows - dist :], "tm", 1)
        return jnp.concatenate([recent, h[: rows - dist]], axis=0)
    if dist == rows:
        return shifted(h, "tm", 1)
    return shifted(h, "tm", dist // rows)


def unlag_rows(moved, dist):
    rows = moved.shape[0]
    if dist < rows:
        local = jnp.concatenate(
            [moved[dist:], jnp.zeros((dist, moved.shape[1]), jnp.float32)], axis=0
        )
        incoming = shifted(moved[:dist].astype(jnp.bfloat16), "tm", -1).astype(jnp.float32)
        return local + jnp.concatenate(
            [jnp.zeros((rows - dist, moved.shape[1]), jnp.float32), incoming], axis=0
        )
    if dist == rows:
        return shifted(moved.astype(jnp.bfloat16), "tm", -1).astype(moved.dtype)
    return shifted(moved.astype(jnp.bfloat16), "tm", -(dist // rows)).astype(moved.dtype)


def conv_pre(h, lagged, taps):
    return jnp.dot(lagged, taps[0], preferred_element_type=jnp.float32) + jnp.dot(
        h, taps[1], preferred_element_type=jnp.float32
    )


def halves(x):
    half = x.shape[0] // 2
    return x[:half], x[half:]


def swapped(x, bit):
    peers = lax.axis_size("tm")
    return lax.ppermute(x, "tm", [(i, i ^ (1 << bit)) for i in range(peers)])


def upper_of(bit):
    return ((lax.axis_index("tm") >> bit) & 1) == 1


def scattered(x, bits):
    for bit in bits:
        low, high = halves(x)
        upper = upper_of(bit)
        got = swapped(jnp.where(upper, low, high), bit)
        kept = jnp.where(upper, high, low)
        x = (kept.astype(jnp.float32) + got.astype(jnp.float32)).astype(jnp.bfloat16)
    return x


def gathered(x, bits):
    for bit in reversed(bits):
        got = swapped(x, bit)
        upper = upper_of(bit)
        x = jnp.concatenate([jnp.where(upper, got, x), jnp.where(upper, x, got)], axis=0)
    return x


def summed(parts, bits):
    peers = lax.axis_size("tm")
    rows = sum(part.shape[0] for part in parts)
    grain = 16 * peers
    spare = -rows % grain
    sent = [part.astype(jnp.bfloat16) for part in parts]
    if spare:
        sent.append(jnp.zeros((spare, parts[0].shape[1]), jnp.bfloat16))
    total = gathered(scattered(jnp.concatenate(sent, axis=0), bits), bits)
    out, at = [], 0
    for part in parts:
        out.append(total[at : at + part.shape[0]].astype(jnp.float32))
        at += part.shape[0]
    return out


def body(stream, w_in, w_conv, w_residual, w_skip, w_out, grad_pred):
    width = w_in.shape[1]
    rows = stream.shape[0]
    layers = w_conv.shape[0]
    skip_width = w_skip.shape[2]
    h = jnp.dot(stream, w_in, preferred_element_type=jnp.float32).astype(jnp.bfloat16)
    skip = jnp.zeros((rows, skip_width), jnp.float32)
    saved = []
    for layer in range(layers):
        dist = rows * 2**layer // 4
        lagged = lag_rows(h, dist)
        z = conv_pre(h, lagged, w_conv[layer])
        gated = (jnp.tanh(z[:, :width]) * jax.nn.sigmoid(z[:, width:])).astype(jnp.bfloat16)
        skip = skip + jnp.dot(gated, w_skip[layer], preferred_element_type=jnp.float32)
        saved.append((h, lagged, z, gated))
        if layer < layers - 1:
            h = (
                h.astype(jnp.float32)
                + jnp.dot(gated, w_residual[layer], preferred_element_type=jnp.float32)
            ).astype(jnp.bfloat16)
    sig_skip = jax.nn.sigmoid(skip)
    active = (skip * sig_skip).astype(jnp.bfloat16)
    prediction = jnp.dot(active, w_out, preferred_element_type=jnp.float32).astype(jnp.bfloat16)
    local_out = tdot(grad_pred, active)
    dact = jnp.dot(grad_pred, w_out.T, preferred_element_type=jnp.float32)
    dskip = (dact * sig_skip * (1.0 + skip * (1.0 - sig_skip))).astype(jnp.bfloat16)
    grad_conv = [None] * layers
    grad_res = [None] * (layers - 1)
    grad_skip = [None] * layers
    dh = None
    for layer in reversed(range(layers)):
        dist = rows * 2**layer // 4
        h_l, lagged, z, gated = saved[layer]
        dg = jnp.dot(dskip, w_skip[layer].T, preferred_element_type=jnp.float32)
        part_skip = tdot(gated, dskip)
        if layer < layers - 1:
            dh_b = dh.astype(jnp.bfloat16)
            dg = dg + jnp.dot(dh_b, w_residual[layer].T, preferred_element_type=jnp.float32)
            grad_res[layer] = tdot(gated, dh_b)
        tanh_part = jnp.tanh(z[:, :width])
        sig_part = jax.nn.sigmoid(z[:, width:])
        dz = jnp.concatenate(
            [
                dg * sig_part * (1.0 - tanh_part * tanh_part),
                dg * tanh_part * sig_part * (1.0 - sig_part),
            ],
            axis=1,
        ).astype(jnp.bfloat16)
        old, new = tdot(lagged, dz), tdot(h_l, dz)
        grad_conv[layer] = [old[:, :width], old[:, width:], new[:, :width], new[:, width:]]
        grad_skip[layer] = part_skip
        new_dh = jnp.dot(dz, w_conv[layer, 1].T, preferred_element_type=jnp.float32) + unlag_rows(
            jnp.dot(dz, w_conv[layer, 0].T, preferred_element_type=jnp.float32), dist
        )
        if layer < layers - 1:
            new_dh = new_dh + dh
        dh = new_dh
    local_in = tdot(stream, dh.astype(jnp.bfloat16))
    bits = list(range((lax.axis_size("tm") - 1).bit_length()))
    other = bits[:1] + bits[2:3] + bits[1:2] + bits[3:]
    mid = layers // 2
    early = summed(
        [part for layer in range(mid, layers) for part in grad_conv[layer]]
        + grad_res[mid:]
        + grad_skip[1:],
        bits,
    )
    late = summed(
        [part for layer in range(mid) for part in grad_conv[layer]]
        + grad_res[:mid]
        + grad_skip[:1]
        + [local_out, local_in],
        other,
    )
    quarters = late[: 4 * mid] + early[: 4 * (layers - mid)]
    early, late = early[4 * (layers - mid) :], late[4 * mid :]
    stacked_conv = jnp.stack(
        [
            jnp.concatenate(quarters[2 * at : 2 * at + 2], axis=1)
            for at in range(2 * layers)
        ]
    ).reshape(layers, 2, width, 2 * width)
    stacked_res = jnp.stack(late[:mid] + early[: layers - 1 - mid])
    stacked_skip = jnp.stack(late[mid : mid + 1] + early[layers - 1 - mid :])
    grad_w_in, grad_w_out = late[-1], late[-2].T
    return (prediction, grad_w_in, stacked_conv, stacked_res, stacked_skip, grad_w_out)


def solution(mesh):
    placed = (P("tm", None), P(), P(), P(), P(), P(), P("tm", None))
    return jax.shard_map(
        body,
        mesh=mesh,
        in_specs=placed,
        out_specs=(P("tm", None), P(), P(), P(), P(), P()),
        check_vma=False,
    )
```

```python
import jax
import jax.numpy as jnp
from jax import lax
from jax.experimental import pallas as pl
from jax.sharding import PartitionSpec as P


def shifted(x, axis, by):
    peers = lax.axis_size(axis)
    pairs = [(i, i + by) for i in range(peers) if 0 <= i + by < peers]
    return lax.ppermute(x, axis, pairs)


def tdot(left, right):
    return lax.dot_general(
        left, right, (((0,), (0,)), ((), ())), preferred_element_type=jnp.float32
    )


def advance_kernel(lag_ref, old_ref, taps_ref, w_ref, out_ref):
    width = old_ref.shape[1]
    old = old_ref[...]
    z = jnp.dot(lag_ref[...], taps_ref[0], preferred_element_type=jnp.float32) + jnp.dot(
        old, taps_ref[1], preferred_element_type=jnp.float32
    )
    gated = (jnp.tanh(z[:, :width]) * jax.nn.sigmoid(z[:, width:])).astype(jnp.bfloat16)
    moved = jnp.dot(gated, w_ref[...], preferred_element_type=jnp.float32)
    out_ref[...] = (old.astype(jnp.float32) + moved).astype(jnp.bfloat16)


def advanced(past, count, dist, taps, w):
    width = past.shape[1]
    step = min(dist, 1024)
    offset = dist // step
    return pl.pallas_call(
        advance_kernel,
        grid=(count // step,),
        in_specs=[
            pl.BlockSpec((step, width), lambda i: (i, 0)),
            pl.BlockSpec((step, width), lambda i: (i + offset, 0)),
            pl.BlockSpec(taps.shape, lambda i: (0, 0, 0)),
            pl.BlockSpec(w.shape, lambda i: (0, 0)),
        ],
        out_specs=pl.BlockSpec((step, width), lambda i: (i, 0)),
        out_shape=jax.ShapeDtypeStruct((count, width), past.dtype),
        cost_estimate=pl.CostEstimate(
            flops=10 * count * width * width,
            bytes_accessed=6 * count * width,
            transcendentals=2 * count * width,
        ),
    )(past, past, taps, w)


def unlag_rows(moved, dist):
    rows = moved.shape[0]
    if dist < rows:
        local = jnp.concatenate(
            [moved[dist:], jnp.zeros((dist, moved.shape[1]), jnp.float32)], axis=0
        )
        incoming = shifted(moved[:dist].astype(jnp.bfloat16), "tm", -1).astype(jnp.float32)
        return local + jnp.concatenate(
            [jnp.zeros((rows - dist, moved.shape[1]), jnp.float32), incoming], axis=0
        )
    if dist == rows:
        return shifted(moved.astype(jnp.bfloat16), "tm", -1).astype(moved.dtype)
    return shifted(moved.astype(jnp.bfloat16), "tm", -(dist // rows)).astype(moved.dtype)


def conv_pre(h, lagged, taps):
    return jnp.dot(lagged, taps[0], preferred_element_type=jnp.float32) + jnp.dot(
        h, taps[1], preferred_element_type=jnp.float32
    )


def halves(x):
    half = x.shape[0] // 2
    return x[:half], x[half:]


def swapped(x, bit):
    peers = lax.axis_size("tm")
    return lax.ppermute(x, "tm", [(i, i ^ (1 << bit)) for i in range(peers)])


def upper_of(bit):
    return ((lax.axis_index("tm") >> bit) & 1) == 1


def scattered(x, bits):
    for bit in bits:
        low, high = halves(x)
        upper = upper_of(bit)
        got = swapped(jnp.where(upper, low, high), bit)
        kept = jnp.where(upper, high, low)
        x = (kept.astype(jnp.float32) + got.astype(jnp.float32)).astype(jnp.bfloat16)
    return x


def gathered(x, bits):
    for bit in reversed(bits):
        got = swapped(x, bit)
        upper = upper_of(bit)
        x = jnp.concatenate([jnp.where(upper, got, x), jnp.where(upper, x, got)], axis=0)
    return x


def summed(parts, bits):
    peers = lax.axis_size("tm")
    rows = sum(part.shape[0] for part in parts)
    grain = 16 * peers
    spare = -rows % grain
    sent = [part.astype(jnp.bfloat16) for part in parts]
    if spare:
        sent.append(jnp.zeros((spare, parts[0].shape[1]), jnp.bfloat16))
    total = gathered(scattered(jnp.concatenate(sent, axis=0), bits), bits)
    out, at = [], 0
    for part in parts:
        out.append(total[at : at + part.shape[0]].astype(jnp.float32))
        at += part.shape[0]
    return out


def body(stream, w_in, w_conv, w_residual, w_skip, w_out, grad_pred):
    width = w_in.shape[1]
    rows = stream.shape[0]
    layers = w_conv.shape[0]
    skip_width = w_skip.shape[2]
    dists = [rows * 2**layer // 4 for layer in range(layers)]
    reach = sum(dists)
    pieces = []
    for back in range(-(-reach // rows), 0, -1):
        want = min(rows, reach - (back - 1) * rows)
        pieces.append(shifted(stream[rows - want :], "tm", back))
    h = jnp.dot(stream, w_in, preferred_element_type=jnp.float32).astype(jnp.bfloat16)
    past = jnp.dot(
        jnp.concatenate(pieces, axis=0), w_in, preferred_element_type=jnp.float32
    ).astype(jnp.bfloat16)
    skip = jnp.zeros((rows, skip_width), jnp.float32)
    saved = []
    for layer in range(layers):
        dist = dists[layer]
        if dist < rows:
            lagged = jnp.concatenate([past[past.shape[0] - dist :], h[: rows - dist]], axis=0)
        elif dist == rows:
            lagged = past[past.shape[0] - rows :]
        else:
            lagged = past
        z = conv_pre(h, lagged, w_conv[layer])
        gated = (jnp.tanh(z[:, :width]) * jax.nn.sigmoid(z[:, width:])).astype(jnp.bfloat16)
        skip = skip + jnp.dot(gated, w_skip[layer], preferred_element_type=jnp.float32)
        saved.append((h, lagged, z, gated))
        if layer < layers - 1:
            count = past.shape[0] - dist
            if layer == layers - 2:
                count = rows
            past = advanced(past, count, dist, w_conv[layer], w_residual[layer])
            h = (
                h.astype(jnp.float32)
                + jnp.dot(gated, w_residual[layer], preferred_element_type=jnp.float32)
            ).astype(jnp.bfloat16)
    sig_skip = jax.nn.sigmoid(skip)
    active = (skip * sig_skip).astype(jnp.bfloat16)
    prediction = jnp.dot(active, w_out, preferred_element_type=jnp.float32).astype(jnp.bfloat16)
    local_out = tdot(grad_pred, active)
    dact = jnp.dot(grad_pred, w_out.T, preferred_element_type=jnp.float32)
    dskip = (dact * sig_skip * (1.0 + skip * (1.0 - sig_skip))).astype(jnp.bfloat16)
    grad_conv = [None] * layers
    grad_res = [None] * (layers - 1)
    grad_skip = [None] * layers
    dh = None
    for layer in reversed(range(layers)):
        dist = rows * 2**layer // 4
        h_l, lagged, z, gated = saved[layer]
        dg = jnp.dot(dskip, w_skip[layer].T, preferred_element_type=jnp.float32)
        part_skip = tdot(gated, dskip)
        if layer < layers - 1:
            dh_b = dh.astype(jnp.bfloat16)
            dg = dg + jnp.dot(dh_b, w_residual[layer].T, preferred_element_type=jnp.float32)
            grad_res[layer] = tdot(gated, dh_b)
        tanh_part = jnp.tanh(z[:, :width])
        sig_part = jax.nn.sigmoid(z[:, width:])
        dz = jnp.concatenate(
            [
                dg * sig_part * (1.0 - tanh_part * tanh_part),
                dg * tanh_part * sig_part * (1.0 - sig_part),
            ],
            axis=1,
        ).astype(jnp.bfloat16)
        old, new = tdot(lagged, dz), tdot(h_l, dz)
        grad_conv[layer] = [old[:, :width], old[:, width:], new[:, :width], new[:, width:]]
        grad_skip[layer] = part_skip
        new_dh = jnp.dot(dz, w_conv[layer, 1].T, preferred_element_type=jnp.float32) + unlag_rows(
            jnp.dot(dz, w_conv[layer, 0].T, preferred_element_type=jnp.float32), dist
        )
        if layer < layers - 1:
            new_dh = new_dh + dh
        dh = new_dh
    local_in = tdot(stream, dh.astype(jnp.bfloat16))
    bits = list(range((lax.axis_size("tm") - 1).bit_length()))
    other = bits[:1] + bits[2:3] + bits[1:2] + bits[3:]
    mid = layers // 2
    early = summed(
        [part for layer in range(mid, layers) for part in grad_conv[layer]]
        + grad_res[mid:]
        + grad_skip[1:],
        bits,
    )
    late = summed(
        [part for layer in range(mid) for part in grad_conv[layer]]
        + grad_res[:mid]
        + grad_skip[:1]
        + [local_out, local_in],
        other,
    )
    quarters = late[: 4 * mid] + early[: 4 * (layers - mid)]
    early, late = early[4 * (layers - mid) :], late[4 * mid :]
    stacked_conv = jnp.stack(
        [
            jnp.concatenate(quarters[2 * at : 2 * at + 2], axis=1)
            for at in range(2 * layers)
        ]
    ).reshape(layers, 2, width, 2 * width)
    stacked_res = jnp.stack(late[:mid] + early[: layers - 1 - mid])
    stacked_skip = jnp.stack(late[mid : mid + 1] + early[layers - 1 - mid :])
    grad_w_in, grad_w_out = late[-1], late[-2].T
    return (prediction, grad_w_in, stacked_conv, stacked_res, stacked_skip, grad_w_out)


def solution(mesh):
    placed = (P("tm", None), P(), P(), P(), P(), P(), P("tm", None))
    return jax.shard_map(
        body,
        mesh=mesh,
        in_specs=placed,
        out_specs=(P("tm", None), P(), P(), P(), P(), P()),
        check_vma=False,
    )
```

```python
import jax
import jax.numpy as jnp
from jax import lax
from jax.experimental import pallas as pl
from jax.experimental.pallas import tpu as pltpu
from jax.sharding import PartitionSpec as P


def shifted(x, axis, by):
    peers = lax.axis_size(axis)
    pairs = [(i, i + by) for i in range(peers) if 0 <= i + by < peers]
    return lax.ppermute(x, axis, pairs)


def tdot(left, right):
    return lax.dot_general(
        left, right, (((0,), (0,)), ((), ())), preferred_element_type=jnp.float32
    )


def advance_kernel(lag_ref, old_ref, taps_ref, w_ref, out_ref):
    width = old_ref.shape[1]
    old = old_ref[...]
    z = jnp.dot(lag_ref[...], taps_ref[0], preferred_element_type=jnp.float32) + jnp.dot(
        old, taps_ref[1], preferred_element_type=jnp.float32
    )
    gated = (jnp.tanh(z[:, :width]) * jax.nn.sigmoid(z[:, width:])).astype(jnp.bfloat16)
    moved = jnp.dot(gated, w_ref[...], preferred_element_type=jnp.float32)
    out_ref[...] = (old.astype(jnp.float32) + moved).astype(jnp.bfloat16)


def advanced(past, count, dist, taps, w):
    width = past.shape[1]
    step = 1024
    old, offset = past, dist // step
    if dist % step:
        old, offset = past[dist:], 0
    return pl.pallas_call(
        advance_kernel,
        grid=(count // step,),
        in_specs=[
            pl.BlockSpec((step, width), lambda i: (i, 0)),
            pl.BlockSpec((step, width), lambda i: (i + offset, 0)),
            pl.BlockSpec(taps.shape, lambda i: (0, 0, 0)),
            pl.BlockSpec(w.shape, lambda i: (0, 0)),
        ],
        out_specs=pl.BlockSpec((step, width), lambda i: (i, 0)),
        out_shape=jax.ShapeDtypeStruct((count, width), past.dtype),
        cost_estimate=pl.CostEstimate(
            flops=10 * count * width * width,
            bytes_accessed=6 * count * width,
            transcendentals=2 * count * width,
        ),
        compiler_params=pltpu.CompilerParams(vmem_limit_bytes=16 * 2**20),
    )(past, old, taps, w)


def unlag_rows(moved, dist):
    rows = moved.shape[0]
    if dist < rows:
        local = jnp.concatenate(
            [moved[dist:], jnp.zeros((dist, moved.shape[1]), jnp.float32)], axis=0
        )
        incoming = shifted(moved[:dist].astype(jnp.bfloat16), "tm", -1).astype(jnp.float32)
        return local + jnp.concatenate(
            [jnp.zeros((rows - dist, moved.shape[1]), jnp.float32), incoming], axis=0
        )
    if dist == rows:
        return shifted(moved.astype(jnp.bfloat16), "tm", -1).astype(moved.dtype)
    return shifted(moved.astype(jnp.bfloat16), "tm", -(dist // rows)).astype(moved.dtype)


def conv_pre(h, lagged, taps):
    return jnp.dot(lagged, taps[0], preferred_element_type=jnp.float32) + jnp.dot(
        h, taps[1], preferred_element_type=jnp.float32
    )


def halves(x):
    half = x.shape[0] // 2
    return x[:half], x[half:]


def swapped(x, bit):
    peers = lax.axis_size("tm")
    return lax.ppermute(x, "tm", [(i, i ^ (1 << bit)) for i in range(peers)])


def upper_of(bit):
    return ((lax.axis_index("tm") >> bit) & 1) == 1


def scattered(x, bits):
    for bit in bits:
        low, high = halves(x)
        upper = upper_of(bit)
        got = swapped(jnp.where(upper, low, high), bit)
        kept = jnp.where(upper, high, low)
        x = (kept.astype(jnp.float32) + got.astype(jnp.float32)).astype(jnp.bfloat16)
    return x


def gathered(x, bits):
    for bit in reversed(bits):
        got = swapped(x, bit)
        upper = upper_of(bit)
        x = jnp.concatenate([jnp.where(upper, got, x), jnp.where(upper, x, got)], axis=0)
    return x


def summed(parts, bits):
    peers = lax.axis_size("tm")
    rows = sum(part.shape[0] for part in parts)
    grain = 16 * peers
    spare = -rows % grain
    sent = [part.astype(jnp.bfloat16) for part in parts]
    if spare:
        sent.append(jnp.zeros((spare, parts[0].shape[1]), jnp.bfloat16))
    total = gathered(scattered(jnp.concatenate(sent, axis=0), bits), bits)
    out, at = [], 0
    for part in parts:
        out.append(total[at : at + part.shape[0]].astype(jnp.float32))
        at += part.shape[0]
    return out


def body(stream, w_in, w_conv, w_residual, w_skip, w_out, grad_pred):
    width = w_in.shape[1]
    rows = stream.shape[0]
    layers = w_conv.shape[0]
    skip_width = w_skip.shape[2]
    dists = [rows * 2**layer // 4 for layer in range(layers)]
    reach = sum(dists)
    pieces = []
    for back in range(-(-reach // rows), 0, -1):
        want = min(rows, reach - (back - 1) * rows)
        pieces.append(shifted(stream[rows - want :], "tm", back))
    h = jnp.dot(stream, w_in, preferred_element_type=jnp.float32).astype(jnp.bfloat16)
    past = jnp.dot(
        jnp.concatenate(pieces, axis=0), w_in, preferred_element_type=jnp.float32
    ).astype(jnp.bfloat16)
    skip = jnp.zeros((rows, skip_width), jnp.float32)
    saved = []
    for layer in range(layers):
        dist = dists[layer]
        if dist < rows:
            lagged = jnp.concatenate([past[past.shape[0] - dist :], h[: rows - dist]], axis=0)
        elif dist == rows:
            lagged = past[past.shape[0] - rows :]
        else:
            lagged = past
        z = conv_pre(h, lagged, w_conv[layer])
        gated = (jnp.tanh(z[:, :width]) * jax.nn.sigmoid(z[:, width:])).astype(jnp.bfloat16)
        skip = skip + jnp.dot(gated, w_skip[layer], preferred_element_type=jnp.float32)
        saved.append((h, lagged, z, gated))
        if layer < layers - 1:
            count = past.shape[0] - dist
            if layer == layers - 2:
                count = rows
            past = advanced(past, count, dist, w_conv[layer], w_residual[layer])
            h = (
                h.astype(jnp.float32)
                + jnp.dot(gated, w_residual[layer], preferred_element_type=jnp.float32)
            ).astype(jnp.bfloat16)
    sig_skip = jax.nn.sigmoid(skip)
    active = (skip * sig_skip).astype(jnp.bfloat16)
    prediction = jnp.dot(active, w_out, preferred_element_type=jnp.float32).astype(jnp.bfloat16)
    local_out = tdot(grad_pred, active)
    dact = jnp.dot(grad_pred, w_out.T, preferred_element_type=jnp.float32)
    dskip = (dact * sig_skip * (1.0 + skip * (1.0 - sig_skip))).astype(jnp.bfloat16)
    grad_conv = [None] * layers
    grad_res = [None] * (layers - 1)
    grad_skip = [None] * layers
    dh = None
    for layer in reversed(range(layers)):
        dist = rows * 2**layer // 4
        h_l, lagged, z, gated = saved[layer]
        dg = jnp.dot(dskip, w_skip[layer].T, preferred_element_type=jnp.float32)
        part_skip = tdot(gated, dskip)
        if layer < layers - 1:
            dh_b = dh.astype(jnp.bfloat16)
            dg = dg + jnp.dot(dh_b, w_residual[layer].T, preferred_element_type=jnp.float32)
            grad_res[layer] = tdot(gated, dh_b)
        tanh_part = jnp.tanh(z[:, :width])
        sig_part = jax.nn.sigmoid(z[:, width:])
        dz = jnp.concatenate(
            [
                dg * sig_part * (1.0 - tanh_part * tanh_part),
                dg * tanh_part * sig_part * (1.0 - sig_part),
            ],
            axis=1,
        ).astype(jnp.bfloat16)
        old, new = tdot(lagged, dz), tdot(h_l, dz)
        grad_conv[layer] = [old[:, :width], old[:, width:], new[:, :width], new[:, width:]]
        grad_skip[layer] = part_skip
        new_dh = jnp.dot(dz, w_conv[layer, 1].T, preferred_element_type=jnp.float32) + unlag_rows(
            jnp.dot(dz, w_conv[layer, 0].T, preferred_element_type=jnp.float32), dist
        )
        if layer < layers - 1:
            new_dh = new_dh + dh
        dh = new_dh
    local_in = tdot(stream, dh.astype(jnp.bfloat16))
    bits = list(range((lax.axis_size("tm") - 1).bit_length()))
    other = bits[:1] + bits[2:3] + bits[1:2] + bits[3:]
    mid = layers // 2
    early = summed(
        [part for layer in range(mid, layers) for part in grad_conv[layer]]
        + grad_res[mid:]
        + grad_skip[1:],
        bits,
    )
    late = summed(
        [part for layer in range(mid) for part in grad_conv[layer]]
        + grad_res[:mid]
        + grad_skip[:1]
        + [local_out, local_in],
        other,
    )
    quarters = late[: 4 * mid] + early[: 4 * (layers - mid)]
    early, late = early[4 * (layers - mid) :], late[4 * mid :]
    stacked_conv = jnp.stack(
        [
            jnp.concatenate(quarters[2 * at : 2 * at + 2], axis=1)
            for at in range(2 * layers)
        ]
    ).reshape(layers, 2, width, 2 * width)
    stacked_res = jnp.stack(late[:mid] + early[: layers - 1 - mid])
    stacked_skip = jnp.stack(late[mid : mid + 1] + early[layers - 1 - mid :])
    grad_w_in, grad_w_out = late[-1], late[-2].T
    return (prediction, grad_w_in, stacked_conv, stacked_res, stacked_skip, grad_w_out)


def solution(mesh):
    placed = (P("tm", None), P(), P(), P(), P(), P(), P("tm", None))
    return jax.shard_map(
        body,
        mesh=mesh,
        in_specs=placed,
        out_specs=(P("tm", None), P(), P(), P(), P(), P()),
        check_vma=False,
    )
```

```python
import jax
import jax.numpy as jnp
from jax import lax
from jax.experimental import pallas as pl
from jax.experimental.pallas import tpu as pltpu
from jax.sharding import PartitionSpec as P


def shifted(x, axis, by):
    peers = lax.axis_size(axis)
    pairs = [(i, i + by) for i in range(peers) if 0 <= i + by < peers]
    return lax.ppermute(x, axis, pairs)


def tdot(left, right):
    return lax.dot_general(
        left, right, (((0,), (0,)), ((), ())), preferred_element_type=jnp.float32
    )


def advance_kernel(lag_ref, old_ref, taps_ref, w_ref, out_ref):
    width = old_ref.shape[1]
    old = old_ref[...]
    z = jnp.dot(lag_ref[...], taps_ref[0], preferred_element_type=jnp.float32) + jnp.dot(
        old, taps_ref[1], preferred_element_type=jnp.float32
    )
    gated = (jnp.tanh(z[:, :width]) * jax.nn.sigmoid(z[:, width:])).astype(jnp.bfloat16)
    moved = jnp.dot(gated, w_ref[...], preferred_element_type=jnp.float32)
    out_ref[...] = (old.astype(jnp.float32) + moved).astype(jnp.bfloat16)


def advanced(past, count, dist, taps, w):
    width = past.shape[1]
    step = 1024
    old, offset = past, dist // step
    if dist % step:
        old, offset = past[dist:], 0
    return pl.pallas_call(
        advance_kernel,
        grid=(count // step,),
        in_specs=[
            pl.BlockSpec((step, width), lambda i: (i, 0)),
            pl.BlockSpec((step, width), lambda i: (i + offset, 0)),
            pl.BlockSpec(taps.shape, lambda i: (0, 0, 0)),
            pl.BlockSpec(w.shape, lambda i: (0, 0)),
        ],
        out_specs=pl.BlockSpec((step, width), lambda i: (i, 0)),
        out_shape=jax.ShapeDtypeStruct((count, width), past.dtype),
        cost_estimate=pl.CostEstimate(
            flops=10 * count * width * width,
            bytes_accessed=6 * count * width,
            transcendentals=2 * count * width,
        ),
        compiler_params=pltpu.CompilerParams(vmem_limit_bytes=16 * 2**20),
    )(past, old, taps, w)


def unlag_rows(moved, dist):
    rows = moved.shape[0]
    if dist < rows:
        local = jnp.concatenate(
            [moved[dist:], jnp.zeros((dist, moved.shape[1]), jnp.float32)], axis=0
        )
        incoming = shifted(moved[:dist].astype(jnp.bfloat16), "tm", -1).astype(jnp.float32)
        return local + jnp.concatenate(
            [jnp.zeros((rows - dist, moved.shape[1]), jnp.float32), incoming], axis=0
        )
    if dist == rows:
        return shifted(moved.astype(jnp.bfloat16), "tm", -1).astype(moved.dtype)
    return shifted(moved.astype(jnp.bfloat16), "tm", -(dist // rows)).astype(moved.dtype)


def conv_pre(h, lagged, taps):
    return jnp.dot(lagged, taps[0], preferred_element_type=jnp.float32) + jnp.dot(
        h, taps[1], preferred_element_type=jnp.float32
    )


def halves(x):
    half = x.shape[0] // 2
    return x[:half], x[half:]


def swapped(x, bit):
    peers = lax.axis_size("tm")
    return lax.ppermute(x, "tm", [(i, i ^ (1 << bit)) for i in range(peers)])


def upper_of(bit):
    return ((lax.axis_index("tm") >> bit) & 1) == 1


def scattered(x, bits):
    for bit in bits:
        low, high = halves(x)
        upper = upper_of(bit)
        got = swapped(jnp.where(upper, low, high), bit)
        kept = jnp.where(upper, high, low)
        x = (kept.astype(jnp.float32) + got.astype(jnp.float32)).astype(jnp.bfloat16)
    return x


def gathered(x, bits):
    for bit in reversed(bits):
        got = swapped(x, bit)
        upper = upper_of(bit)
        x = jnp.concatenate([jnp.where(upper, got, x), jnp.where(upper, x, got)], axis=0)
    return x


def summed(parts, bits):
    peers = lax.axis_size("tm")
    rows = sum(part.shape[0] for part in parts)
    grain = 16 * peers
    spare = -rows % grain
    sent = [part.astype(jnp.bfloat16) for part in parts]
    if spare:
        sent.append(jnp.zeros((spare, parts[0].shape[1]), jnp.bfloat16))
    total = gathered(scattered(jnp.concatenate(sent, axis=0), bits), bits)
    out, at = [], 0
    for part in parts:
        out.append(total[at : at + part.shape[0]].astype(jnp.float32))
        at += part.shape[0]
    return out


def body(stream, w_in, w_conv, w_residual, w_skip, w_out, grad_pred):
    width = w_in.shape[1]
    rows = stream.shape[0]
    layers = w_conv.shape[0]
    skip_width = w_skip.shape[2]
    dists = [rows * 2**layer // 4 for layer in range(layers)]
    reach = sum(dists)
    pieces = []
    for back in range(-(-reach // rows), 0, -1):
        want = min(rows, reach - (back - 1) * rows)
        pieces.append(shifted(stream[rows - want :], "tm", back))
    h = jnp.dot(stream, w_in, preferred_element_type=jnp.float32).astype(jnp.bfloat16)
    past = jnp.dot(
        jnp.concatenate(pieces, axis=0), w_in, preferred_element_type=jnp.float32
    ).astype(jnp.bfloat16)
    skip = jnp.zeros((rows, skip_width), jnp.float32)
    saved = []
    for layer in range(layers):
        dist = dists[layer]
        if dist < rows:
            lagged = jnp.concatenate([past[past.shape[0] - dist :], h[: rows - dist]], axis=0)
        elif dist == rows:
            lagged = past[past.shape[0] - rows :]
        else:
            lagged = past
        z = conv_pre(h, lagged, w_conv[layer])
        gated = (jnp.tanh(z[:, :width]) * jax.nn.sigmoid(z[:, width:])).astype(jnp.bfloat16)
        skip = skip + jnp.dot(gated, w_skip[layer], preferred_element_type=jnp.float32)
        saved.append((h, lagged, z, gated))
        if layer < layers - 1:
            count = past.shape[0] - dist
            if layer == layers - 2:
                count = rows
            past = advanced(past, count, dist, w_conv[layer], w_residual[layer])
            h = (
                h.astype(jnp.float32)
                + jnp.dot(gated, w_residual[layer], preferred_element_type=jnp.float32)
            ).astype(jnp.bfloat16)
    sig_skip = jax.nn.sigmoid(skip)
    active = (skip * sig_skip).astype(jnp.bfloat16)
    prediction = jnp.dot(active, w_out, preferred_element_type=jnp.float32).astype(jnp.bfloat16)
    local_out = tdot(grad_pred, active)
    dact = jnp.dot(grad_pred, w_out.T, preferred_element_type=jnp.float32)
    dskip = (dact * sig_skip * (1.0 + skip * (1.0 - sig_skip))).astype(jnp.bfloat16)
    grad_conv = [None] * layers
    grad_res = [None] * (layers - 1)
    grad_skip = [None] * layers
    dh = None
    for layer in reversed(range(layers)):
        dist = rows * 2**layer // 4
        h_l, lagged, z, gated = saved[layer]
        dg = jnp.dot(dskip, w_skip[layer].T, preferred_element_type=jnp.float32)
        part_skip = tdot(gated, dskip)
        if layer < layers - 1:
            dh_b = dh.astype(jnp.bfloat16)
            dg = dg + jnp.dot(dh_b, w_residual[layer].T, preferred_element_type=jnp.float32)
            grad_res[layer] = tdot(gated, dh_b)
        tanh_part = jnp.tanh(z[:, :width])
        sig_part = jax.nn.sigmoid(z[:, width:])
        dz = jnp.concatenate(
            [
                dg * sig_part * (1.0 - tanh_part * tanh_part),
                dg * tanh_part * sig_part * (1.0 - sig_part),
            ],
            axis=1,
        ).astype(jnp.bfloat16)
        old, new = tdot(lagged, dz), tdot(h_l, dz)
        grad_conv[layer] = [old[:, :width], old[:, width:], new[:, :width], new[:, width:]]
        grad_skip[layer] = part_skip
        new_dh = jnp.dot(dz, w_conv[layer, 1].T, preferred_element_type=jnp.float32) + unlag_rows(
            jnp.dot(dz, w_conv[layer, 0].T, preferred_element_type=jnp.float32), dist
        )
        if layer < layers - 1:
            new_dh = new_dh + dh
        dh = new_dh
    local_in = tdot(stream, dh.astype(jnp.bfloat16))
    bits = list(range((lax.axis_size("tm") - 1).bit_length()))
    other = bits[:1] + bits[2:3] + bits[1:2] + bits[3:]
    last = layers - 1
    first_sum = summed(grad_conv[last] + grad_skip, bits)
    second = summed(
        [part for layer in range(1, last) for part in grad_conv[layer]] + grad_res[1:], other
    )
    third = summed(grad_conv[0] + grad_res[:1] + [local_out, local_in], bits)
    cut = 4 * (last - 1)
    quarters = third[:4] + second[:cut] + first_sum[:4]
    stacked_conv = jnp.stack(
        [
            jnp.concatenate(quarters[2 * at : 2 * at + 2], axis=1)
            for at in range(2 * layers)
        ]
    ).reshape(layers, 2, width, 2 * width)
    stacked_res = jnp.stack(third[4:5] + second[cut:])
    stacked_skip = jnp.stack(first_sum[4:])
    grad_w_in, grad_w_out = third[-1], third[-2].T
    return (prediction, grad_w_in, stacked_conv, stacked_res, stacked_skip, grad_w_out)


def solution(mesh):
    placed = (P("tm", None), P(), P(), P(), P(), P(), P("tm", None))
    return jax.shard_map(
        body,
        mesh=mesh,
        in_specs=placed,
        out_specs=(P("tm", None), P(), P(), P(), P(), P()),
        check_vma=False,
    )
```
